32 devices in a mesh: dp: 8 (over z, y), tensor: 4 (over x, core).
Axes of the slice: x: 2, y: 2, z: 4, core: 2. Of those that a mesh axis runs over, the one named last changes fastest.
Arguments:
- tokens: bfloat16 [16384, 1024], P(('dp', 'tensor')), may hold values from -6 to 6
- ln_gain: float32 [1024], replicated, may hold values from 0.1 to 1.9
- ln_bias: float32 [1024], replicated, may hold values from -1.75 to 1.75
- w_qkv: bfloat16 [3, 1024, 16, 64], P(None, None, 'tensor'), may hold values from -0.1875 to 0.1875
- b_qkv: float32 [3, 16, 64], P(None, 'tensor'), may hold values from -3 to 3
- w_in: bfloat16 [1024, 4096], P(None, 'tensor'), may hold values from -0.1875 to 0.1875
- b_in: float32 [4096], P('tensor'), may hold values from -3 to 3
- w_out: bfloat16 [16, 64, 1024], P('tensor'), may hold values from -1.5 to 1.5
- w_down: bfloat16 [4096, 1024], P('tensor'), may hold values from -0.09375 to 0.09375
- b_out: float32 [1024], replicated, may hold values from -3 to 3
- cotangent: bfloat16 [16384, 1024], P(('dp', 'tensor')), may hold values from -6 to 6
- block_doc: int32 [8, 4], P('dp'), may hold values from 0 to 2, as said below
Outputs:
- block_out: bfloat16 [16384, 1024], P(('dp', 'tensor'))
- grad_tokens: float32 [16384, 1024], P(('dp', 'tensor'))
- grad_ln_gain: float32 [1024], replicated
- grad_ln_bias: float32 [1024], replicated
- grad_w_qkv: float32 [3, 1024, 16, 64], P(None, 'dp', 'tensor')
- grad_b_qkv: float32 [3, 16, 64], replicated
- grad_w_in: float32 [1024, 4096], P('dp', 'tensor')
- grad_b_in: float32 [4096], replicated
- grad_w_out: float32 [16, 64, 1024], P('tensor', None, 'dp')
- grad_w_down: float32 [4096, 1024], P('tensor', 'dp')
- grad_b_out: float32 [1024], replicated
The draws below stay inside these ranges and needn't reach their ends.
Inputs may be any that keep to these rules, and one draw needn't show every extreme that they name: `block_doc`: in each group the numbers start at 0 and rise by 0 or 1 from block to block. Every sequence covers a power of two of blocks, at most 2; a sequence of k blocks starts at a block index divisible by k; each group has a sequence of exactly 2 blocks.
All inputs are finite; a program needn't handle non-finite values.
Results may differ from the reference program's by a relative error of at most 0.012.
The reference program's roundings to bfloat16 on the way count: a program that leaves them out, or rounds other values in their place, can miss the bound.
Values may be sent and summed in bfloat16 or wider, within the bound.
No kernel may reach another device: no remote copies, remote signals or barrier semaphores. Data moves between devices by JAX's collectives and lax.ppermute only.
A program may use at most 256 MiB of HBM per device.

```python
import jax
import jax.numpy as jnp
from jax import lax

D = 1024
HEADS = 16
HD = 64
FF = 4096
ROT = 16
BLK = 512
GROUP = 2048
NB = 4
SEQB = 2
TOKENS = 16384
N_DP = 8


def draw_block_doc(key, part):
    level_sizes = []
    size_now = SEQB
    while size_now > 1:
        level_sizes.append(size_now)
        size_now = size_now // 2
    key_prob, key_levels = jax.random.split(key)
    threshold = jax.random.randint(key_prob, (N_DP, 1), 1, 10)
    block_ids = jnp.arange(NB, dtype=jnp.int32)
    lengths = jnp.ones((N_DP, NB), jnp.int32)
    decided = jnp.zeros((N_DP, NB), dtype=jnp.bool_)
    for level_index, level_size in enumerate(level_sizes):
        dice_rolls = jax.random.randint(jax.random.fold_in(key_levels, level_index), (N_DP, NB // level_size), 0, 10)
        chosen = dice_rolls < threshold
        if level_size == SEQB:
            chosen = chosen.at[:, 0].set(True)
        chosen = jnp.repeat(chosen, level_size, axis=1)
        lengths = jnp.where(chosen & jnp.logical_not(decided), level_size, lengths)
        decided = decided | chosen
    begins = block_ids[None, :] % lengths == 0
    return (jnp.cumsum(begins.astype(jnp.int32), axis=1) - 1).astype(jnp.int32)


def with_spikes(result, rng, source, target, blocks, factor):
    def block_of(position):
        return (jnp.arange(result.shape[position]) // (result.shape[position] // blocks)).reshape((-1,) + (1,) * (result.ndim - 1 - position))

    first = jax.random.permutation(rng, blocks)[block_of(target)]
    other_side = (block_of(target) + blocks // 2) % blocks
    return jnp.where((block_of(source) == first) | (block_of(source) == other_side), factor * result, result)


def block_scale(own_key, extent, shards, least, high):
    factor_of, own = 1.0, jax.random.fold_in(own_key, 6)
    for axis_at, parts in shards:
        draws = jnp.exp(jax.random.uniform(jax.random.fold_in(own, axis_at), (parts,), jnp.float32, least / len(shards), high / len(shards)))
        factor_of = factor_of * jnp.repeat(draws, extent[axis_at] // parts).reshape([-1 if axis == axis_at else 1 for axis in range(len(extent))])
    return factor_of


def normal_values(key, dims, width, bound, shards=(), kind=jnp.bfloat16):
    result = jax.random.normal(key, dims, jnp.float32) * width
    if len(shards) > 0:
        result = block_scale(key, dims, shards, -0.22, 0.18) * result
    return jnp.clip(result, min=-bound, max=bound).astype(kind)


def noise_with(rng, extent, deviation, bound, cuts, heavy, kind=jnp.bfloat16):
    result = deviation * jax.random.normal(rng, extent, jnp.float32)
    if cuts:
        result = result * block_scale(rng, extent, cuts, -0.22, 0.18)
    return jnp.clip(with_spikes(result, jax.random.fold_in(rng, 3), *heavy), -bound, bound).astype(kind)


def setup_inputs(seed: int = 0) -> dict:
    arg_keys = jax.random.split(jax.random.key(seed), 13)
    return {
        "tokens": normal_values(arg_keys[0], (TOKENS, D), 1.0, 6.0, ((0, 32),)),
        "ln_gain": jnp.clip(1.0 + 0.18 * jax.random.normal(arg_keys[1], (D,), jnp.float32), 0.1, 1.9),
        "ln_bias": normal_values(arg_keys[2], (D,), 0.3, 1.75, (), jnp.float32),
        "w_qkv": normal_values(arg_keys[3], (3, D, HEADS, HD), D ** -0.5, 0.1875, ((2, 4),)),
        "b_qkv": normal_values(arg_keys[4], (3, HEADS, HD), 0.5, 3.0, ((1, 4),), jnp.float32),
        "w_in": normal_values(arg_keys[5], (D, FF), D ** -0.5, 0.1875, ((1, 4),)),
        "b_in": normal_values(arg_keys[6], (FF,), 0.5, 3.0, ((0, 4),), jnp.float32),
        "w_out": normal_values(arg_keys[7], (HEADS, HD, D), 16 ** -0.5, 1.5, ((0, 4),)),
        "w_down": normal_values(arg_keys[8], (FF, D), FF ** -0.5, 0.09375, ((0, 4),)),
        "b_out": normal_values(arg_keys[9], (D,), 0.5, 3.0, (), jnp.float32),
        "cotangent": noise_with(arg_keys[10], (TOKENS, D), 1.0, 6.0, ((0, 32),), (0, 1, 32, 2.75)),
        "block_doc": draw_block_doc(jax.random.fold_in(arg_keys[12], 71), 0),
    }


epsilon = 1e-05
highest = lax.Precision.HIGHEST

@jax.custom_vjp
def low(v):
    return lax.optimization_barrier(v.astype(jnp.bfloat16)).astype(jnp.float32)

@jax.custom_vjp
def low_back(v):
    return v

def low_keep(v):
    return (low(v), None)

def low_pass(kept, grad):
    return (grad,)

def back_keep(v):
    return (v, None)

def back_low(kept, grad):
    return (low(grad),)
low.defvjp(low_keep, low_pass)
low_back.defvjp(back_keep, back_low)

def layer_norm(rows, ln_gain, ln_bias):
    mean_row = lax.optimization_barrier(jnp.mean(rows, axis=-1, keepdims=True))
    centred = rows - mean_row
    var_row = lax.optimization_barrier(jnp.mean(centred * centred, axis=-1, keepdims=True))
    return centred * lax.rsqrt(var_row + epsilon) * ln_gain + ln_bias

def rope_tables(positions):
    half_dims = ROT // 2
    inverse = 1.0 / 10000.0 ** (jnp.arange(half_dims, dtype=jnp.float32) * 2.0 / ROT)
    angles = positions[:, None] * inverse[None, :]
    return (jnp.cos(angles), jnp.sin(angles))

def rotate(vectors, cosine_table, sine_table):
    half_dims = ROT // 2
    leading = vectors[..., :half_dims]
    trailing = vectors[..., half_dims:ROT]
    remain = vectors[..., ROT:]
    cosine = cosine_table[:, None, :]
    sine = sine_table[:, None, :]
    return jnp.concatenate([leading * cosine - trailing * sine, trailing * cosine + leading * sine, remain], axis=-1)

def attention(queries, all_keys, all_values, group_docs):
    score_scale = HD ** (-0.5)
    pad_rows = (SEQB - 1) * BLK
    keys_padded = jnp.concatenate([jnp.zeros((pad_rows, HEADS, HD), jnp.float32), all_keys], axis=0)
    values_padded = jnp.concatenate([jnp.zeros((pad_rows, HEADS, HD), jnp.float32), all_values], axis=0)
    padded_docs = jnp.concatenate([jnp.full((SEQB - 1,), -1, jnp.int32), group_docs])
    key_docs = jnp.repeat(padded_docs, BLK)

    def one_block(query_block):
        first_row = query_block * BLK
        query_rows = lax.dynamic_slice_in_dim(queries, first_row, BLK, 0)
        key_rows = lax.dynamic_slice_in_dim(keys_padded, first_row, SEQB * BLK, 0)
        value_rows = lax.dynamic_slice_in_dim(values_padded, first_row, SEQB * BLK, 0)
        window_docs = lax.dynamic_slice_in_dim(key_docs, first_row, SEQB * BLK, 0)
        query_pos = first_row + jnp.arange(BLK, dtype=jnp.int32)
        key_pos = first_row - pad_rows + jnp.arange(SEQB * BLK, dtype=jnp.int32)
        allowed = (window_docs[None, :] == group_docs[query_block]) & (key_pos[None, :] <= query_pos[:, None])
        scores = low_back(jnp.einsum('qhe,khe->hqk', query_rows, key_rows, precision=highest) * score_scale)
        scores = jnp.where(allowed[None], scores, -1e+30)
        weights = low(jax.nn.softmax(scores, axis=-1))
        return jnp.einsum('hqk,khe->qhe', weights, value_rows, precision=highest)
    blocks = lax.map(jax.checkpoint(one_block), jnp.arange(NB, dtype=jnp.int32))
    return blocks.reshape(GROUP, HEADS, HD)

def group_forward(group_tokens, group_docs, ln_gain, ln_bias, w_qkv, b_qkv, w_in, b_in, w_out, w_down, b_out):
    normed = low(layer_norm(group_tokens, ln_gain, ln_bias))
    projected = [low_back(jnp.einsum('td,dhe->the', normed, w_qkv[member], precision=highest) + b_qkv[member]) for member in range(3)]
    hidden_pre = low_back(jnp.dot(normed, w_in, precision=highest) + b_in)
    block_starts = lax.optimization_barrier(jnp.sum((group_docs[None, :] < group_docs[:, None]).astype(jnp.int32), axis=1))
    positions = (jnp.arange(GROUP, dtype=jnp.int32) - jnp.repeat(block_starts, BLK) * BLK).astype(jnp.float32)
    cosine_table, sine_table = rope_tables(positions)
    queries = low(rotate(projected[0], cosine_table, sine_table))
    all_keys = low(rotate(projected[1], cosine_table, sine_table))
    all_values = low(projected[2])
    attended = low_back(low(attention(queries, all_keys, all_values, group_docs)))
    active = low(jax.nn.gelu(hidden_pre, approximate=False))
    mixed = jnp.einsum('the,hed->td', attended, w_out, precision=highest) + jnp.dot(active, w_down, precision=highest)
    return group_tokens + mixed + b_out

def reference(tokens, ln_gain, ln_bias, w_qkv, b_qkv, w_in, b_in, w_out, w_down, b_out, cotangent, block_doc):
    token_groups = tokens.astype(jnp.float32).reshape(N_DP, GROUP, D)
    params = (ln_gain.astype(jnp.float32), ln_bias.astype(jnp.float32), w_qkv.astype(jnp.float32), b_qkv.astype(jnp.float32), w_in.astype(jnp.float32), b_in.astype(jnp.float32), w_out.astype(jnp.float32), w_down.astype(jnp.float32), b_out.astype(jnp.float32))

    def whole(token_groups, *weights):

        def scan_step(carried, scanned):
            group_tokens, group_docs = scanned
            return (carried, jax.checkpoint(group_forward)(group_tokens, group_docs, *weights))
        _, outputs = lax.scan(scan_step, jnp.zeros((), jnp.float32), (token_groups, block_doc))
        return outputs
    outputs, pullback = jax.vjp(whole, token_groups, *params)
    grads = pullback(cotangent.astype(jnp.float32).reshape(N_DP, GROUP, D))
    return (outputs.reshape(TOKENS, D).astype(jnp.bfloat16), grads[0].reshape(TOKENS, D), grads[1], grads[2], grads[3], grads[4], grads[5], grads[6], grads[7], grads[8], grads[9])
```

```python
from functools import partial

import jax
import jax.numpy as jnp
from jax import lax
from jax.experimental import pallas as pl
from jax.experimental.pallas import tpu as pltpu
from jax.sharding import PartitionSpec as P

ROT = 16
BLK = 512
epsilon = 1e-05


f32 = jnp.float32
bf16 = jnp.bfloat16

NN = (((1,), (0,)), ((), ()))
NT = (((1,), (1,)), ((), ()))
TN = (((0,), (0,)), ((), ()))


def mm(a, b, dims):
    return lax.dot_general(a, b, dims, preferred_element_type=f32)


def params(mib=56):
    return pltpu.CompilerParams(vmem_limit_bytes=mib << 20)


def cost(flops, bytes_accessed, transcendentals=0):
    return pl.CostEstimate(
        flops=int(flops), bytes_accessed=int(bytes_accessed), transcendentals=int(transcendentals)
    )


def moments(rows):
    mean_row = jnp.mean(rows, axis=-1, keepdims=True)
    centred = rows - mean_row
    var_row = jnp.mean(centred * centred, axis=-1, keepdims=True)
    return centred, lax.rsqrt(var_row + epsilon)


def norm_body(tok_ref, cot_ref, gain_ref, bias_ref, out_ref, sum_ref):
    centred, inv = moments(tok_ref[...].astype(f32))
    out_ref[...] = (centred * inv * gain_ref[...] + bias_ref[...]).astype(bf16)
    part = jnp.sum(cot_ref[...].astype(f32), axis=0, keepdims=True)

    @pl.when(pl.program_id(0) == 0)
    def _():
        sum_ref[...] = jnp.zeros_like(sum_ref)

    sum_ref[...] += part


def norm_forward(tokens, cotangent, gain, bias):
    rows, width = tokens.shape
    tile = 128
    row = pl.BlockSpec((tile, width), lambda i: (i, 0))
    one = pl.BlockSpec((1, width), lambda i: (0, 0))
    return pl.pallas_call(
        norm_body,
        grid=(rows // tile,),
        in_specs=[row, row, one, one],
        out_specs=[row, one],
        out_shape=[
            jax.ShapeDtypeStruct((rows, width), bf16),
            jax.ShapeDtypeStruct((1, width), f32),
        ],
        compiler_params=params(),
        cost_estimate=cost(10 * rows * width, 6 * rows * width),
        name="norm_forward",
    )(tokens, cotangent, gain, bias)


def rope_lanes(window, lanes, head_dim):
    half = ROT // 2
    inverse = 1.0 / 10000.0 ** (jnp.arange(half, dtype=f32) * 2.0 / ROT)
    angles = inverse[:, None] * jnp.arange(window, dtype=f32)[None, :]
    cosine, sine = jnp.cos(angles).T, jnp.sin(angles).T
    rest = jnp.ones((window, head_dim - ROT), f32)
    zero = jnp.zeros((window, half), f32)
    zrest = jnp.zeros((window, head_dim - half), f32)
    heads = lanes // head_dim
    plain = jnp.concatenate([cosine, cosine, rest] * heads, axis=1)
    from_up = jnp.concatenate([-sine, zrest] * heads, axis=1)
    from_down = jnp.concatenate([zero, sine, rest * 0.0] * heads, axis=1)
    return plain, from_up, from_down


def shift_lanes(x, amount):
    lanes = x.shape[1]
    amount = amount % lanes
    if lanes % 128 == 0:
        return pltpu.roll(x, amount, 1)
    return jnp.concatenate([x[:, lanes - amount :], x[:, : lanes - amount]], axis=1)


def rope(x, plain, from_up, from_down):
    return x * plain + shift_lanes(x, -8) * from_up + shift_lanes(x, 8) * from_down


def heads_body(cols, lanes, pb_ref, n_ref, c_ref, w_ref, wo_ref, b_ref, t0, t1, t2, q, k, v, go):
    rows = n_ref[...]
    plain, up, down = t0[...], t1[...], t2[...]
    for member, out in enumerate((q, k, v)):
        pre = mm(rows, w_ref[member * cols : (member + 1) * cols, :], NT)
        pre = pre + b_ref[:, member * cols : (member + 1) * cols]
        if member < 2:
            pre = jnp.concatenate(
                [
                    rope(pre[:, at : at + lanes], plain, up, down)
                    for at in range(0, cols, lanes)
                ],
                axis=1,
            )
        out[...] = pre.astype(bf16)
    go[...] = mm(c_ref[...], wo_ref[...], NT).astype(bf16)


def project_heads(normed, cot, w_t, w_out, bias, tables, pos_blocks):
    rows, width = normed.shape
    cols = w_out.shape[0]
    lanes = tables[0].shape[1]
    tile = 256
    per = BLK // tile
    row = pl.BlockSpec((tile, width), lambda i, pb: (i, 0))
    whole = lambda a: pl.BlockSpec(a.shape, lambda i, pb: (0, 0))
    tab = pl.BlockSpec((tile, lanes), lambda i, pb: (pb[i // per] * per + i % per, 0))
    out = pl.BlockSpec((tile, cols), lambda i, pb: (i, 0))
    return pl.pallas_call(
        partial(heads_body, cols, lanes),
        grid_spec=pltpu.PrefetchScalarGridSpec(
            num_scalar_prefetch=1,
            grid=(rows // tile,),
            in_specs=[row, row, whole(w_t), whole(w_out), whole(bias), tab, tab, tab],
            out_specs=[out] * 4,
        ),
        out_shape=[jax.ShapeDtypeStruct((rows, cols), bf16)] * 4,
        compiler_params=params(),
        cost_estimate=cost(
            8 * rows * width * cols, 4 * rows * width + 8 * width * cols + 8 * rows * cols
        ),
        name="project_heads",
    )(pos_blocks, normed, cot, w_t, w_out, bias, *tables)


def ffn_body(sub, n_ref, c_ref, wi_ref, wd_ref, b_ref, act, gh, gb):
    r, f = pl.program_id(0), pl.program_id(1)
    total = jnp.zeros(b_ref.shape, f32)
    for at in range(0, n_ref.shape[0], sub):
        part = slice(at, at + sub)
        h = mm(n_ref[part, :], wi_ref[...], NN) + b_ref[...]
        g = mm(c_ref[part, :], wd_ref[...], NT)
        cdf = 0.5 * (1.0 + lax.erf(h * 0.7071067811865476))
        pdf = 0.3989422804014327 * jnp.exp(-0.5 * h * h)
        act[part, :] = (h * cdf).astype(bf16)
        low = (g * (cdf + h * pdf)).astype(bf16)
        gh[part, :] = low
        total = total + jnp.sum(low.astype(f32), axis=0, keepdims=True)

    @pl.when(r == 0)
    def _():
        gb[f] = total

    @pl.when(r != 0)
    def _():
        gb[f] = gb[f] + total


def feed_forward(normed, cot, w_in, w_down, b_in):
    rows, width = normed.shape
    hidden = w_in.shape[1]
    tile, ft = 512, min(256, hidden)
    row = pl.BlockSpec((tile, width), lambda r, f: (r, 0))
    out = pl.BlockSpec((tile, ft), lambda r, f: (r, f))
    act, gh, gb = pl.pallas_call(
        partial(ffn_body, 128),
        grid=(rows // tile, hidden // ft),
        in_specs=[
            row,
            row,
            pl.BlockSpec((width, ft), lambda r, f: (0, f)),
            pl.BlockSpec((ft, width), lambda r, f: (f, 0)),
            pl.BlockSpec((1, ft), lambda r, f: (0, f)),
        ],
        out_specs=[out, out, pl.BlockSpec((hidden // ft, 1, ft), lambda r, f: (0, 0, 0))],
        out_shape=[
            jax.ShapeDtypeStruct((rows, hidden), bf16),
            jax.ShapeDtypeStruct((rows, hidden), bf16),
            jax.ShapeDtypeStruct((hidden // ft, 1, ft), f32),
        ],
        compiler_params=params(),
        cost_estimate=cost(
            4 * rows * width * hidden + 50 * rows * hidden,
            4 * rows * width + 4 * width * hidden + 4 * rows * hidden,
            2 * rows * hidden,
        ),
        name="feed_forward",
    )(normed, cot, w_in, w_down, b_in)
    return act, gh, gb.reshape(hidden)


def attention_body(
    blocks, head_dim, doc_ref, pb_ref, q_ref, k_ref, v_ref, go_ref, t0, t1, t2,
    out_ref, dq_ref, dk_ref, dv_ref, gb_ref, acck, accv,
):
    window, lanes = q_ref.shape
    heads = lanes // head_dim
    base = pl.program_id(0) * blocks
    scale = head_dim**-0.5
    qt = 256
    keys, values = k_ref[...], v_ref[...]
    keys_t = keys.astype(f32).T.astype(bf16)
    values_t = values.astype(f32).T.astype(bf16)
    lane = lax.broadcasted_iota(jnp.int32, (qt, lanes), 1)
    causal = lax.broadcasted_iota(jnp.int32, (qt, qt), 0) <= lax.broadcasted_iota(
        jnp.int32, (qt, qt), 1
    )
    acck[...] = jnp.zeros_like(acck)
    accv[...] = jnp.zeros_like(accv)

    def tables(block):
        rows = pl.ds(pl.multiple_of(pb_ref[base + block] * BLK, BLK), BLK)
        return t0[rows, :], -t1[rows, :], -t2[rows, :]

    sums = []
    for block in range(blocks):
        plain, up, down = tables(block)
        mine = doc_ref[base + block]
        for half in range(BLK // qt):
            first = block * BLK + half * qt
            length = first + qt
            q_tile, go_tile = q_ref[first:length, :], go_ref[first:length, :]
            lows, grads, qs, gos, outs, dqs = [], [], [], [], [], []
            for head in range(heads):
                own = (lane >= head * head_dim) & (lane < (head + 1) * head_dim)
                qm = jnp.where(own, q_tile.astype(f32) * scale, 0.0).astype(bf16)
                gm = jnp.where(own, go_tile.astype(f32), 0.0).astype(bf16)
                scores = mm(keys[:length, :], qm, NT)
                pieces = []
                for other in range(block):
                    bias = jnp.where(doc_ref[base + other] == mine, 0.0, -1e30).astype(f32)
                    pieces.append(scores[other * BLK : (other + 1) * BLK, :] + bias)
                if half:
                    pieces.append(scores[block * BLK : first, :])
                pieces.append(jnp.where(causal, scores[first:length, :], -1e30))
                scores = jnp.concatenate(pieces, axis=0) if len(pieces) > 1 else pieces[0]
                top = jnp.max(scores, axis=0, keepdims=True)
                weights = jnp.exp(scores - top)
                weights = weights * (1.0 / jnp.sum(weights, axis=0, keepdims=True))
                gw = mm(values[:length, :], gm, NT)
                delta = jnp.sum(weights * gw, axis=0, keepdims=True)
                low = weights.astype(bf16)
                gs = (weights * (gw - delta)).astype(bf16)
                rows = slice(head * head_dim, (head + 1) * head_dim)
                outs.append(mm(values_t[rows, :length], low, NN))
                dqs.append(mm(keys_t[rows, :length], gs, NN))
                lows.append(low)
                grads.append(gs)
                qs.append(qm)
                gos.append(gm)
            cat = lambda parts, axis: (
                jnp.concatenate(parts, axis=axis) if len(parts) > 1 else parts[0]
            )
            out_ref[first:length, :] = cat(outs, 0).T.astype(bf16)
            accv[:length, :] += mm(cat(lows, 1), cat(gos, 0), NN)
            acck[:length, :] += mm(cat(grads, 1), cat(qs, 0), NN)
            dq = cat(dqs, 0).T * scale
            rows = slice(half * qt, (half + 1) * qt)
            dq = rope(dq, plain[rows], up[rows], down[rows]).astype(bf16)
            dq_ref[first:length, :] = dq
            sums.append(jnp.sum(dq.astype(f32), axis=0, keepdims=True))
    sums_k = []
    for block in range(blocks):
        rows = slice(block * BLK, (block + 1) * BLK)
        dk = rope(acck[rows, :], *tables(block)).astype(bf16)
        dk_ref[rows, :] = dk
        sums_k.append(jnp.sum(dk.astype(f32), axis=0, keepdims=True))
    dv = accv[...].astype(bf16)
    dv_ref[...] = dv
    gb_ref[0, 0] = sum(sums)
    gb_ref[0, 1] = sum(sums_k)
    gb_ref[0, 2] = jnp.sum(dv.astype(f32), axis=0, keepdims=True)


def attention(q, k, v, go, tables, docs, pos_blocks, blocks, head_dim):
    rows, cols = q.shape
    lanes = tables[0].shape[1]
    window = blocks * BLK
    wins = rows // window
    part = pl.BlockSpec((window, lanes), lambda w, h, d, p: (w, h))
    tab = pl.BlockSpec((window, lanes), lambda w, h, d, p: (0, 0))
    pairs = wins * (cols // head_dim) * window * window * 0.6
    out, dq, dk, dv, gb = pl.pallas_call(
        partial(attention_body, blocks, head_dim),
        grid_spec=pltpu.PrefetchScalarGridSpec(
            num_scalar_prefetch=2,
            grid=(wins, cols // lanes),
            in_specs=[part] * 4 + [tab] * 3,
            out_specs=[part] * 4
            + [pl.BlockSpec((1, 3, 1, lanes), lambda w, h, d, p: (w, 0, 0, h))],
            scratch_shapes=[pltpu.VMEM((window, lanes), f32)] * 2,
        ),
        out_shape=[jax.ShapeDtypeStruct((rows, cols), bf16)] * 4
        + [jax.ShapeDtypeStruct((wins, 3, 1, cols), f32)],
        compiler_params=params(),
        cost_estimate=cost(40 * pairs * head_dim, 16 * rows * cols, pairs),
        name="attention",
    )(docs, pos_blocks, q, k, v, go, *tables)
    return out, dq, dk, dv, jnp.sum(gb, axis=0)[:, 0, :]


def branch_body(rhs_dims, split, half_ref, *refs):
    count = len(rhs_dims)
    total = None
    for at, dims in enumerate(rhs_dims):
        term = mm(refs[at][...], refs[count + at][...], dims)
        total = term if total is None else total + term
    total = total.astype(bf16)
    if not split:
        refs[2 * count][...] = total
        return
    which = pl.program_id(0)

    @pl.when(which == 0)
    def _():
        refs[2 * count][...] = total

    @pl.when(which != 0)
    def _():
        refs[2 * count + 1][...] = total


def branch_sum(lefts, rights, rhs_dims, half=None):
    rows = lefts[0].shape[0]
    width = rights[0].shape[1] if rhs_dims[0] == NN else rights[0].shape[0]
    tile = 256
    split = half is not None
    halves = 2 if split else 1
    per = rows // halves // tile
    half = jnp.zeros((1,), jnp.int32) if half is None else half.reshape(1).astype(jnp.int32)
    if split:
        row = lambda h, i, s: (jnp.where(h == 0, 1 - s[0], s[0]) * per + i, 0)
        out_specs = [
            pl.BlockSpec((tile, width), lambda h, i, s: (jnp.where(h == 0, i, per - 1), 0)),
            pl.BlockSpec((tile, width), lambda h, i, s: (jnp.where(h == 0, 0, i), 0)),
        ]
    else:
        row = lambda h, i, s: (i, 0)
        out_specs = [pl.BlockSpec((tile, width), lambda h, i, s: (i, 0))]
    depth = sum(a.shape[1] for a in lefts)
    outs = pl.pallas_call(
        partial(branch_body, rhs_dims, split),
        grid_spec=pltpu.PrefetchScalarGridSpec(
            num_scalar_prefetch=1,
            grid=(halves, per),
            in_specs=[pl.BlockSpec((tile, a.shape[1]), row) for a in lefts]
            + [pl.BlockSpec(b.shape, lambda h, i, s: (0, 0)) for b in rights],
            out_specs=out_specs,
        ),
        out_shape=[jax.ShapeDtypeStruct((rows // halves, width), bf16)] * halves,
        compiler_params=params(),
        cost_estimate=cost(
            2 * rows * width * depth, 2 * depth * (rows + width) + 2 * rows * width
        ),
        name="branch_sum",
    )(half, *lefts, *rights)
    return outs if split else outs[0]


def send_order(bits):
    kept = [0]
    groups = [[0]]
    for bit in reversed(bits):
        sent = [p ^ bit for p in kept]
        groups.insert(0, sent)
        kept = sent + kept
    return groups


def weight_body(counts, plan, by_rows, sizes, pos_ref, *refs):
    chunks = len(counts)
    slots = len({i for i, _ in plan} | {j for _, j in plan})
    ins = refs[: chunks * slots]
    outs = refs[chunks * slots : -1]
    acc = refs[-1]
    step = pl.program_id(0)
    start = 0
    for chunk, count in enumerate(counts):
        mine = ins[chunk * slots : (chunk + 1) * slots]

        @pl.when((step >= start) & (step < start + count))
        def _(mine=mine):
            at = 0
            for left, right in plan:
                lref, rref = mine[left], mine[right]
                n = lref.shape[1]
                sub = min(256, n)
                for j in range(0, n, sub):
                    term = mm(lref[:, j : j + sub], rref[...], TN)
                    rows = slice(at + j, at + j + sub)
                    acc[rows, :] = jnp.where(step == 0, 0.0, acc[rows, :]) + term
                at += n

        start += count

    @pl.when(step == start - 1)
    def _():
        total = acc.shape[0] if by_rows else acc.shape[1]
        parts = sum(sizes)
        size = total // parts
        for block in range(parts):
            span = slice(block * size, (block + 1) * size)
            at = pos_ref[block]
            value = (acc[span, :] if by_rows else acc[:, span]).astype(bf16)
            low = 0
            for out, number in zip(outs, sizes):

                @pl.when((at >= low) & (at < low + number))
                def _(out=out, low=low):
                    out[at - low] = value

                low += number


def weight_grad(chunks, plan, by_rows, positions, sizes):
    tile = 512
    counts = [c[0].shape[0] // tile for c in chunks]
    acc_rows = sum(chunks[0][i].shape[1] for i, _ in plan)
    acc_cols = chunks[0][plan[0][1]].shape[1]
    parts = sum(sizes)
    block = (acc_rows // parts, acc_cols) if by_rows else (acc_rows, acc_cols // parts)
    in_specs, start = [], 0
    for arrays, count in zip(chunks, counts):
        for a in arrays:
            in_specs.append(
                pl.BlockSpec(
                    (tile, a.shape[1]),
                    lambda s, pos, start=start, count=count: (
                        jnp.clip(s - start, 0, count - 1),
                        0,
                    ),
                )
            )
        start += count
    tokens = sum(c[0].shape[0] for c in chunks)
    return pl.pallas_call(
        partial(weight_body, counts, plan, by_rows, sizes),
        grid_spec=pltpu.PrefetchScalarGridSpec(
            num_scalar_prefetch=1,
            grid=(start,),
            in_specs=in_specs,
            out_specs=[
                pl.BlockSpec((n,) + block, lambda s, pos: (0, 0, 0)) for n in sizes
            ],
            scratch_shapes=[pltpu.VMEM((acc_rows, acc_cols), f32)],
        ),
        out_shape=[jax.ShapeDtypeStruct((n,) + block, bf16) for n in sizes],
        compiler_params=params(),
        cost_estimate=cost(
            2 * tokens * acc_rows * acc_cols,
            2 * tokens * (acc_rows + acc_cols) + 2 * acc_rows * acc_cols,
        ),
        name="weight_grad",
    )(positions, *[a for c in chunks for a in c])


def norm_back_body(count, tok_ref, cot_ref, gain_ref, *refs):
    grads, (out_ref, gsum, bsum) = refs[:count], refs[count:]
    centred, inv = moments(tok_ref[...].astype(f32))
    xhat = centred * inv
    gn = sum(g[...].astype(f32) for g in grads)
    e = gain_ref[...] * gn
    mean_e = jnp.mean(e, axis=-1, keepdims=True)
    mean_ex = jnp.mean(e * xhat, axis=-1, keepdims=True)
    out_ref[...] = cot_ref[...].astype(f32) + inv * (e - mean_e - xhat * mean_ex)

    @pl.when(pl.program_id(0) == 0)
    def _():
        gsum[...] = jnp.zeros_like(gsum)
        bsum[...] = jnp.zeros_like(bsum)

    gsum[...] += jnp.sum(gn * xhat, axis=0, keepdims=True)
    bsum[...] += jnp.sum(gn, axis=0, keepdims=True)


def norm_backward(tokens, cotangent, gain, grads):
    rows, width = tokens.shape
    tile = 128
    row = pl.BlockSpec((tile, width), lambda i: (i, 0))
    one = pl.BlockSpec((1, width), lambda i: (0, 0))
    return pl.pallas_call(
        partial(norm_back_body, len(grads)),
        grid=(rows // tile,),
        in_specs=[row, row, one] + [row] * len(grads),
        out_specs=[row, one, one],
        out_shape=[
            jax.ShapeDtypeStruct((rows, width), f32),
            jax.ShapeDtypeStruct((1, width), f32),
            jax.ShapeDtypeStruct((1, width), f32),
        ],
        compiler_params=params(),
        cost_estimate=cost(20 * rows * width, 14 * rows * width),
        name="norm_backward",
    )(tokens, cotangent, gain, *grads)


def swap(value, axis, bit):
    return lax.ppermute(value, axis, [(i, i ^ bit) for i in range(lax.axis_size(axis))])


def bits_of(size):
    return [1 << i for i in range(size.bit_length() - 1)]


def after(value, *first):
    return lax.optimization_barrier((value,) + first)[0]


def sum_over(value, axis):
    for bit in bits_of(lax.axis_size(axis)):
        value = value + swap(value, axis, bit)
    return value


def halve(groups, axis, bits):
    arrays = list(groups)
    for step, bit in enumerate(bits):
        got = swap(arrays[0], axis, bit)
        rest, at = [], 0
        last = step == len(bits) - 1
        for array in arrays[1:]:
            n = array.shape[0]
            total = array.astype(f32) + got[at : at + n].astype(f32)
            rest.append(total if last else total.astype(bf16))
            at += n
        arrays = rest
    return arrays[0][0]


def shards(
    tokens, ln_gain, ln_bias, w_qkv, b_qkv, w_in, b_in, w_out, w_down, b_out, cotangent, block_doc
):
    rows_local, width = tokens.shape
    heads, head_dim = w_qkv.shape[2], w_qkv.shape[3]
    cols = heads * head_dim
    hidden = w_in.shape[1]
    n_tensor, n_dp = lax.axis_size("tensor"), lax.axis_size("dp")
    t_rank, d_rank = lax.axis_index("tensor"), lax.axis_index("dp")
    docs = block_doc[0]
    num_blocks = docs.shape[0]
    seq_blocks = min(4, num_blocks // 2)
    starts = jnp.sum((docs[None, :] < docs[:, None]).astype(jnp.int32), axis=1)
    pos_blocks = jnp.arange(num_blocks, dtype=jnp.int32) - starts
    paired = n_tensor == 4 and seq_blocks == 2 and rows_local == BLK
    core = t_rank % 2
    lanes = min(128, cols)

    gain, bias = ln_gain.reshape(1, width), ln_bias.reshape(1, width)
    w_t = jnp.transpose(w_qkv, (0, 2, 3, 1)).reshape(3 * cols, width)
    wo = w_out.reshape(cols, width)
    normed, bout_part = norm_forward(tokens, cotangent, gain, bias)
    tables = rope_lanes(seq_blocks * BLK, lanes, head_dim)

    def pair(mine, other):
        return jnp.where(
            core == 0,
            jnp.concatenate([mine, other], axis=0),
            jnp.concatenate([other, mine], axis=0),
        )

    if paired:
        cot_far = swap(cotangent, "tensor", 2)
        normed_far = swap(normed, "tensor", 2)
        cots = [
            pair(cotangent, swap(cotangent, "tensor", 1)),
            pair(cot_far, swap(cot_far, "tensor", 1)),
        ]
        normeds = [
            pair(normed, swap(normed, "tensor", 1)),
            pair(normed_far, swap(normed_far, "tensor", 1)),
        ]
        chip = t_rank // 2
        chunk_docs = [
            (lax.dynamic_slice(a, (2 * chip,), (2,)), lax.dynamic_slice(a, (2 - 2 * chip,), (2,)))
            for a in (docs, pos_blocks)
        ]
        chunk_docs = list(zip(*chunk_docs))
    else:
        cots = [lax.all_gather(cotangent, "tensor", axis=0, tiled=True)]
        normeds = [lax.all_gather(normed, "tensor", axis=0, tiled=True)]
        chunk_docs = [(docs, pos_blocks)]
    chunks = len(cots)
    half = core if paired else None

    bits = bits_of(n_dp)
    turned = bits[1:] + bits[:1]

    def weights(arrays, plan, by_rows, order):
        groups = send_order(order)
        sequence = [p for g in groups for p in g]
        place = jnp.asarray([sequence.index(p) for p in range(n_dp)], jnp.int32)
        mine = place[jnp.arange(n_dp, dtype=jnp.int32) ^ d_rank]
        blocks = weight_grad(arrays, plan, by_rows, mine, [len(g) for g in groups])
        return halve(blocks, "dp", order)

    b_heads = b_qkv.reshape(1, 3 * cols)
    b_hidden = b_in.reshape(1, hidden)
    acts, ghs, gb_in = [], [], 0.0
    for i in range(chunks):
        act, gh, gb = feed_forward(normeds[i], cots[i], w_in, w_down, b_hidden)
        acts.append(act)
        ghs.append(gh)
        gb_in = gb_in + gb
    grad_w_down = weights(list(zip(acts, cots)), [(0, 1)], False, bits)
    grad_w_in = weights(list(zip(normeds, ghs)), [(0, 1)], True, turned)

    mixes, gns, heads_out, gb_heads = [], [], [], 0.0
    for i in range(chunks):
        q, k, v, go = project_heads(
            normeds[i], cots[i], w_t, wo, b_heads, tables, chunk_docs[i][1]
        )
        att, dq, dk, dv, gb = attention(
            q, k, v, go, tables, *chunk_docs[i], seq_blocks, head_dim
        )
        gb_heads = gb_heads + gb
        heads_out.append((dq, dk, dv, att))
        mixes.append(branch_sum([att, acts[i]], [wo, w_down], [NN, NN], half))
        gns.append(
            branch_sum(
                [dq, dk, dv, ghs[i]],
                [w_t[:cols], w_t[cols : 2 * cols], w_t[2 * cols :], w_in],
                [NN, NN, NN, NT],
                half,
            )
        )
    grad_w_heads = weights(
        [(*h, n, c) for h, n, c in zip(heads_out, normeds, cots)],
        [(0, 4), (1, 4), (2, 4), (3, 5)],
        False,
        bits,
    )

    def terms(parts):
        if not paired:
            full = lax.psum_scatter(parts[0], "tensor", scatter_dimension=0, tiled=True)
            return [full]
        (send_near, near), (send_far, far) = parts
        far = far.astype(f32) + swap(send_far, "tensor", 1).astype(f32)
        return [near, swap(send_near, "tensor", 1), swap(far.astype(bf16), "tensor", 2)]

    mixed = sum(a.astype(f32) for a in terms(mixes))
    block_out = (tokens.astype(f32) + mixed + b_out).astype(bf16)
    grad_tokens, gain_part, bias_part = norm_backward(tokens, cotangent, gain, terms(gns))

    early = jnp.concatenate([gb_in, gb_heads.reshape(3 * cols)])
    early = sum_over(early, "dp")
    early = lax.all_gather(early, "tensor", axis=0) if not paired else gather_small(early)
    grad_b_in = early[:, :hidden].reshape(n_tensor * hidden)
    grad_b_qkv = (
        early[:, hidden:]
        .reshape(n_tensor, 3, heads, head_dim)
        .transpose(1, 0, 2, 3)
        .reshape(3, n_tensor * heads, head_dim)
    )
    late = jnp.concatenate([gain_part[0], bias_part[0], bout_part[0]])
    late = sum_over(sum_over(late, "dp"), "tensor")
    return (
        block_out,
        grad_tokens,
        late[:width],
        late[width : 2 * width],
        grad_w_heads[: 3 * cols].reshape(3, heads, head_dim, -1).transpose(0, 3, 1, 2),
        grad_b_qkv,
        grad_w_in,
        grad_b_in,
        grad_w_heads[3 * cols :].reshape(heads, head_dim, -1),
        grad_w_down,
        late[2 * width :],
    )


def gather_small(value):
    rank = lax.axis_index("tensor")
    rows = value[None]
    for bit in bits_of(lax.axis_size("tensor")):
        got = swap(rows, "tensor", bit)
        rows = jnp.where(
            rank & bit == 0,
            jnp.concatenate([rows, got], axis=0),
            jnp.concatenate([got, rows], axis=0),
        )
    return rows


def solution(mesh):
    return jax.shard_map(
        shards,
        mesh=mesh,
        in_specs=(
            P(("dp", "tensor"), None),
            P(),
            P(),
            P(None, None, "tensor", None),
            P(None, "tensor", None),
            P(None, "tensor"),
            P("tensor"),
            P("tensor", None, None),
            P("tensor", None),
            P(),
            P(("dp", "tensor"), None),
            P("dp", None),
        ),
        out_specs=(
            P(("dp", "tensor"), None),
            P(("dp", "tensor"), None),
            P(),
            P(),
            P(None, "dp", "tensor", None),
            P(),
            P("dp", "tensor"),
            P(),
            P("tensor", None, "dp"),
            P("tensor", "dp"),
            P(),
        ),
        check_vma=False,
    )
```
